32 devices in a mesh: row: 8 (over y, x, core), col: 4 (over z).
Axes of the slice: x: 2, y: 2, z: 4, core: 2. Of those that a mesh axis runs over, the one named last changes fastest.
Arguments:
- act_tiles: bfloat16 [3072, 2048], P('row', 'col'), may hold values from -6 to 6
- up_tiles: bfloat16 [2048, 3584], P('row', 'col'), may hold values from -0.125 to 0.125
Outputs:
- hidden_act: bfloat16 [3072, 3584], P('row', 'col')
The draws below stay inside these ranges and needn't reach their ends.
All inputs are finite; a program needn't handle non-finite values.
Results may differ from the reference program's by a relative error of at most 0.001.
Values may be sent and summed in bfloat16 or wider, within the bound.
A program may use at most 64 MiB of HBM per device.

```python
import jax
import jax.numpy as jnp
from jax import lax

TOK_DEV = 384
KB = 256
HID_DEV = 896
D = 2048
TOKENS = 3072
FF = 3584
N_ROW = 8
N_COL = 4


def shard_levels(own_key, shape, split, smallest, top_value):
    factor_of = 1.0
    for axis_at, parts in split:
        draws = jax.random.uniform(jax.random.fold_in(jax.random.fold_in(own_key, 6), axis_at), (parts,), jnp.float32, smallest / len(split), top_value / len(split))
        factor_of = factor_of * jnp.repeat(jnp.exp(draws), shape[axis_at] // parts).reshape((-1,) + (1,) * (len(shape) - 1 - axis_at))
    return factor_of


def bell_draw(key, dims, deviation, most, cuts=(), held_as=jnp.bfloat16):
    drawn = deviation * jax.random.normal(key, dims, jnp.float32)
    if cuts:
        drawn = drawn * shard_levels(key, dims, cuts, -0.22, 0.18)
    return jnp.clip(drawn, -most, most).astype(held_as)


def setup_inputs(seed: int = 0) -> dict:
    streams_of = jax.random.split(jax.random.key(seed), 3)
    act_tiles = bell_draw(streams_of[0], (TOKENS, D), 1.0, 6.0, ((0, 8), (1, 4)))
    up_tiles = bell_draw(streams_of[1], (D, FF), D ** -0.5, 0.125, ((0, 8), (1, 4)))
    return dict(act_tiles=act_tiles, up_tiles=up_tiles)


def reference(act_tiles, up_tiles):
    block_ids = jnp.arange(N_ROW, dtype=jnp.int32)
    act_blocks = act_tiles.reshape(N_ROW, TOK_DEV, N_ROW, KB)

    def unskew_row(blocks, row_index):
        return jnp.take(blocks, (block_ids - row_index) % N_ROW, axis=1)

    features = jax.vmap(unskew_row)(act_blocks, block_ids).reshape(N_ROW * TOK_DEV, N_ROW * KB).astype(jnp.float32)
    up_blocks = up_tiles.reshape(N_ROW, KB, N_COL, HID_DEV)

    def column_block(col_index):
        column = lax.dynamic_index_in_dim(up_blocks, col_index, 2, keepdims=False)
        weights = jnp.take(column, (block_ids - 2 * col_index) % N_ROW, axis=0).reshape(N_ROW * KB, HID_DEV).astype(jnp.float32)
        pre = jnp.dot(features, weights, preferred_element_type=jnp.float32, precision=lax.Precision.HIGHEST)
        return jax.nn.silu(pre).astype(jnp.bfloat16)

    result = lax.map(column_block, jnp.arange(N_COL, dtype=jnp.int32))
    return jnp.transpose(result, (1, 0, 2)).reshape(N_ROW * TOK_DEV, N_COL * HID_DEV)
```

```python
import functools

import jax
import jax.numpy as jnp
from jax import lax
from jax.experimental import pallas as pl
from jax.experimental.pallas import tpu as pltpu
from jax.sharding import PartitionSpec as P

MESH = pl.DeviceIdType.MESH


def pieces_of(rows, wanted, multiple):
    return max(n for n in range(1, wanted + 1) if rows % (n * multiple) == 0)


def kernel(grid, counts, a_hbm, w_hbm, out, acts, weights, total, send_a, recv_a, send_w, recv_w, local_sem):
    n_y, n_x, n_col = grid
    n_a, n_w = counts
    n_row = 2 * n_y * n_x
    tokens, width = acts.shape[1:]
    depth = w_hbm.shape[0]
    per = width // depth
    row_a, row_w = tokens // n_a, depth // n_w

    r, c = lax.axis_index("row"), lax.axis_index("col")
    core = lax.rem(r, 2)
    x = lax.rem(r // 2, n_x)
    y = r // (2 * n_x)
    last = n_col - 1

    def row_of(dy, dx, other_core=False):
        which = 1 - core if other_core else core
        return (lax.rem(y + dy, n_y) * n_x + lax.rem(x + dx, n_x)) * 2 + which

    pair = row_of(0, 0, True)
    peers_x = [(0, dx) for dx in range(1, n_x)]
    peers_y = [(dy, 0) for dy in range(1, n_y)]
    diagonal = [(dy, dx) for dy in range(1, n_y) for dx in range(1, n_x)]

    def weight_at(source, owner, k):
        rel = lax.rem(source - owner + n_row, n_row)
        return weights.at[rel // per, pl.ds(pl.multiple_of(lax.rem(rel, per) * depth + k * row_w, row_w), row_w)]

    def weight_copy(source, to, slot, k):
        return pltpu.make_async_remote_copy(
            src_ref=weight_at(source, r, k),
            dst_ref=weight_at(source, to, k),
            send_sem=send_w.at[slot, k],
            recv_sem=recv_w.at[source, k],
            device_id=(to, c),
            device_id_type=MESH,
        )

    def act_copy(source, side, k):
        return pltpu.make_async_remote_copy(
            src_ref=acts.at[source, pl.ds(k * row_a, row_a)],
            dst_ref=acts.at[source, pl.ds(k * row_a, row_a)],
            send_sem=send_a.at[side, source, k],
            recv_sem=recv_a.at[source, k],
            device_id=(r, c + 2 * side - 1),
            device_id_type=MESH,
        )

    own_a = pltpu.make_async_copy(a_hbm, acts.at[c], local_sem.at[0])
    own_w = pltpu.make_async_copy(w_hbm, weights.at[0, pl.ds(0, depth)], local_sem.at[1])
    own_a.start()
    own_w.start()

    barrier = pltpu.get_barrier_semaphore()
    row_peers = [row_of(*p) for p in peers_x + peers_y] + [pair]
    for to in row_peers:
        pl.semaphore_signal(barrier, inc=1, device_id=(to, c), device_id_type=MESH)

    @pl.when(c > 0)
    def _():
        pl.semaphore_signal(barrier, inc=1, device_id=(r, c - 1), device_id_type=MESH)

    @pl.when(c < last)
    def _():
        pl.semaphore_signal(barrier, inc=1, device_id=(r, c + 1), device_id_type=MESH)

    beside = jnp.where(c > 0, 1, 0) + jnp.where(c < last, 1, 0)
    pl.semaphore_wait(barrier, len(row_peers) + beside)

    own_a.wait()

    def own_acts(k, act):
        @pl.when(c < last)
        def _():
            act(act_copy(c, 1, k))

        @pl.when(c > 0)
        def _():
            act(act_copy(c, 0, k))

    for k in range(n_a):
        own_acts(k, lambda copy: copy.start())
    own_w.wait()
    for k in range(n_w):
        for slot, to in enumerate(row_peers):
            weight_copy(r, to, slot, k).start()

    near = [row_of(*p) for p in peers_x + peers_y]
    far = [row_of(*p) for p in diagonal]
    base_relay = len(row_peers)
    base_share = base_relay + len(diagonal)

    def relays(k, act):
        for n, (dy, dx) in enumerate(diagonal):
            @pl.when(core == 0)
            def _():
                act(weight_copy(row_of(dy, 0), row_of(0, dx), base_relay + n, k))

            @pl.when(core == 1)
            def _():
                act(weight_copy(row_of(0, dx), row_of(dy, 0), base_relay + n, k))

    def wait_weight(source, k):
        weight_copy(source, r, 0, k).wait_recv()

    def first_weights(k):
        for source in near:
            wait_weight(source, k)
        relays(k, lambda copy: copy.start())
        for n, source in enumerate(near):
            weight_copy(source, pair, base_share + n, k).start()

    def far_weights(k):
        for n, source in enumerate(far):
            wait_weight(source, k)
            weight_copy(source, pair, base_share + len(near) + n, k).start()

    short = jnp.minimum(c, last - c)
    toward = jnp.where(last - c >= c, 1, -1)

    def source_at(t):
        near_step = t // 2 + 1
        near_sign = toward * (1 - 2 * lax.rem(t, 2))
        return jnp.where(t < 2 * short, c + near_sign * near_step, c + toward * (t - short + 1))

    inner = jnp.logical_and(c > 0, c < last)

    def pass_acts(t, k):
        source = source_at(t)
        act_copy(source, 0, k).wait_recv()

        @pl.when(source < c)
        def _():
            act_copy(source, 1, k).start()

        @pl.when(source > c)
        def _():
            act_copy(source, 0, k).start()

    events = []
    a_time, w_time = row_a * width, row_w * weights.shape[2]
    for t in range(last):
        for k in range(n_a):
            events.append(((t // 2 * n_a + k + 1) * a_time, "a", t, k))
    for k in range(n_w):
        events.append(((k + 1) * w_time * (n_x + n_y - 2) / 2, "near", 0, k))
        events.append(((k + 2) * w_time * (n_x + n_y - 2) / 2 + w_time, "far", 0, k))
    for _, kind, t, k in sorted(events):
        if kind == "a":
            pl.when(inner)(functools.partial(pass_acts, t, k))
        elif kind == "near":
            first_weights(k)
        else:
            far_weights(k)
    for k in range(n_w):
        for source in [pair] + [row_of(dy, dx, True) for dy, dx in peers_x + peers_y + diagonal]:
            wait_weight(source, k)

    def product(source, rows):
        at = lax.rem(source - c + n_col, n_col)
        return jnp.dot(acts[source, rows, :], weights[at], preferred_element_type=jnp.float32)

    every = pl.ds(0, tokens)
    total[...] = product(c, every)

    @pl.loop(0, last - 1)
    def _(t):
        source = source_at(t)

        @pl.when(jnp.logical_not(inner))
        def _():
            for k in range(n_a):
                act_copy(source, 0, k).wait_recv()

        total[...] += product(source, every)

    final = source_at(last - 1)

    @pl.loop(0, n_a)
    def _(k):
        rows = pl.ds(pl.multiple_of(k * row_a, row_a), row_a)

        @pl.when(jnp.logical_not(inner))
        def _():
            act_copy(final, 0, k).wait_recv()

        pre = total[rows, :] + product(final, rows)
        out[rows, :] = (pre / (1.0 + jnp.exp(-pre))).astype(out.dtype)

    for k in range(n_a):
        own_acts(k, lambda copy: copy.wait_send())

    @pl.when(inner)
    def _():
        @pl.loop(0, last)
        def _(t):
            source = source_at(t)
            for k in range(n_a):
                @pl.when(source < c)
                def _():
                    act_copy(source, 1, k).wait_send()

                @pl.when(source > c)
                def _():
                    act_copy(source, 0, k).wait_send()

    for k in range(n_w):
        for slot, to in enumerate(row_peers):
            weight_copy(r, to, slot, k).wait_send()
        relays(k, lambda copy: copy.wait_send())
        for n, source in enumerate(near + far):
            weight_copy(source, pair, base_share + n, k).wait_send()


def body(n_row, n_col, act_tiles, up_tiles):
    tokens, width = act_tiles.shape
    depth, hidden = up_tiles.shape
    chips = n_row // 2
    n_x = max(n for n in range(1, chips + 1) if chips % n == 0 and n * n <= chips)
    n_y = chips // n_x
    n_a, n_w = pieces_of(tokens, 4, 16), pieces_of(depth, 2, 16)
    sends = (n_x - 1) + (n_y - 1) + 1 + (n_x - 1) * (n_y - 1) + chips - 1
    return pl.pallas_call(
        functools.partial(kernel, (n_y, n_x, n_col), (n_a, n_w)),
        out_shape=jax.ShapeDtypeStruct((tokens, hidden), jnp.bfloat16),
        in_specs=[pl.BlockSpec(memory_space=pltpu.HBM)] * 2,
        out_specs=pl.BlockSpec(memory_space=pltpu.VMEM),
        scratch_shapes=[
            pltpu.VMEM((n_col, tokens, width), jnp.bfloat16),
            pltpu.VMEM((n_row * depth // width, width, hidden), jnp.bfloat16),
            pltpu.VMEM((tokens, hidden), jnp.float32),
            pltpu.SemaphoreType.DMA((2, n_col, n_a)),
            pltpu.SemaphoreType.DMA((n_col, n_a)),
            pltpu.SemaphoreType.DMA((sends, n_w)),
            pltpu.SemaphoreType.DMA((n_row, n_w)),
            pltpu.SemaphoreType.DMA((2,)),
        ],
        compiler_params=pltpu.CompilerParams(collective_id=0, has_side_effects=True, vmem_limit_bytes=48 << 20),
        cost_estimate=pl.CostEstimate(
            flops=2 * tokens * width * n_col * hidden,
            bytes_accessed=2 * (act_tiles.size + up_tiles.size + tokens * hidden),
            transcendentals=tokens * hidden,
        ),
        name="gather_up_silu",
    )(act_tiles, up_tiles)


def solution(mesh):
    return jax.shard_map(
        functools.partial(body, mesh.shape["row"], mesh.shape["col"]),
        mesh=mesh,
        in_specs=(P("row", "col"), P("row", "col")),
        out_specs=P("row", "col"),
        check_vma=False,
    )
```

```python
import functools

import jax
import jax.numpy as jnp
from jax import lax
from jax.experimental import pallas as pl
from jax.experimental.pallas import tpu as pltpu
from jax.sharding import PartitionSpec as P

MESH = pl.DeviceIdType.MESH


def pieces_of(rows, wanted, multiple):
    return max(n for n in range(1, wanted + 1) if rows % (n * multiple) == 0)


def kernel(grid, counts, a_hbm, w_hbm, out, acts, weights, total, send_a, recv_a, send_w, recv_w, local_sem):
    n_y, n_x, n_col = grid
    n_a, n_w = counts
    n_row = 2 * n_y * n_x
    tokens, width = acts.shape[1:]
    depth = w_hbm.shape[0]
    per = width // depth
    row_a, row_w = tokens // n_a, depth // n_w

    r, c = lax.axis_index("row"), lax.axis_index("col")
    core = lax.rem(r, 2)
    x = lax.rem(r // 2, n_x)
    y = r // (2 * n_x)
    last = n_col - 1

    def row_of(dy, dx, other_core=False):
        which = 1 - core if other_core else core
        return (lax.rem(y + dy, n_y) * n_x + lax.rem(x + dx, n_x)) * 2 + which

    pair = row_of(0, 0, True)
    peers_x = [(0, dx) for dx in range(1, n_x)]
    peers_y = [(dy, 0) for dy in range(1, n_y)]
    diagonal = [(dy, dx) for dy in range(1, n_y) for dx in range(1, n_x)]

    def weight_at(source, owner, k):
        rel = lax.rem(source - owner + n_row, n_row)
        return weights.at[rel // per, pl.ds(pl.multiple_of(lax.rem(rel, per) * depth + k * row_w, row_w), row_w)]

    def weight_copy(source, to, slot, k, own=False):
        return pltpu.make_async_remote_copy(
            src_ref=w_hbm.at[pl.ds(k * row_w, row_w)] if own else weight_at(source, r, k),
            dst_ref=weight_at(source, to, k),
            send_sem=send_w.at[slot, k],
            recv_sem=recv_w.at[source, k],
            device_id=(to, c),
            device_id_type=MESH,
        )

    def act_copy(source, side, k, own=False):
        return pltpu.make_async_remote_copy(
            src_ref=(a_hbm if own else acts.at[source]).at[pl.ds(k * row_a, row_a)],
            dst_ref=acts.at[source, pl.ds(k * row_a, row_a)],
            send_sem=send_a.at[side, source, k],
            recv_sem=recv_a.at[source, k],
            device_id=(r, c + 2 * side - 1),
            device_id_type=MESH,
        )

    own_a = pltpu.make_async_copy(a_hbm, acts.at[c], local_sem.at[0])
    own_w = pltpu.make_async_copy(w_hbm, weights.at[0, pl.ds(0, depth)], local_sem.at[1])
    own_a.start()
    own_w.start()

    barrier = pltpu.get_barrier_semaphore()
    row_peers = [row_of(*p) for p in peers_x + peers_y] + [pair]
    for to in row_peers:
        pl.semaphore_signal(barrier, inc=1, device_id=(to, c), device_id_type=MESH)

    @pl.when(c > 0)
    def _():
        pl.semaphore_signal(barrier, inc=1, device_id=(r, c - 1), device_id_type=MESH)

    @pl.when(c < last)
    def _():
        pl.semaphore_signal(barrier, inc=1, device_id=(r, c + 1), device_id_type=MESH)

    beside = jnp.where(c > 0, 1, 0) + jnp.where(c < last, 1, 0)
    pl.semaphore_wait(barrier, len(row_peers) + beside)

    def own_acts(k, act):
        @pl.when(c < last)
        def _():
            act(act_copy(c, 1, k, True))

        @pl.when(c > 0)
        def _():
            act(act_copy(c, 0, k, True))

    for k in range(n_a):
        own_acts(k, lambda copy: copy.start())
    for k in range(n_w):
        for slot, to in enumerate(row_peers):
            weight_copy(r, to, slot, k, True).start()

    near = [row_of(*p) for p in peers_x + peers_y]
    far = [row_of(*p) for p in diagonal]
    base_relay = len(row_peers)
    base_share = base_relay + len(diagonal)

    def relays(k, act):
        for n, (dy, dx) in enumerate(diagonal):
            @pl.when(core == 0)
            def _():
                act(weight_copy(row_of(dy, 0), row_of(0, dx), base_relay + n, k))

            @pl.when(core == 1)
            def _():
                act(weight_copy(row_of(0, dx), row_of(dy, 0), base_relay + n, k))

    def wait_weight(source, k):
        weight_copy(source, r, 0, k).wait_recv()

    def first_weights(k):
        for source in near:
            wait_weight(source, k)
        relays(k, lambda copy: copy.start())
        for n, source in enumerate(near):
            weight_copy(source, pair, base_share + n, k).start()

    def far_weights(k):
        for n, source in enumerate(far):
            wait_weight(source, k)
            weight_copy(source, pair, base_share + len(near) + n, k).start()

    short = jnp.minimum(c, last - c)
    toward = jnp.where(last - c >= c, 1, -1)

    def source_at(t):
        near_step = t // 2 + 1
        near_sign = toward * (1 - 2 * lax.rem(t, 2))
        return jnp.where(t < 2 * short, c + near_sign * near_step, c + toward * (t - short + 1))

    inner = jnp.logical_and(c > 0, c < last)

    def pass_acts(t, k):
        source = source_at(t)
        act_copy(source, 0, k).wait_recv()

        @pl.when(source < c)
        def _():
            act_copy(source, 1, k).start()

        @pl.when(source > c)
        def _():
            act_copy(source, 0, k).start()

    events = []
    a_time, w_time = row_a * width, row_w * weights.shape[2]
    for t in range(last):
        for k in range(n_a):
            events.append(((t // 2 * n_a + k + 1) * a_time, "a", t, k))
    for k in range(n_w):
        events.append(((k + 1) * w_time * (n_x + n_y - 2) / 2, "near", 0, k))
        events.append(((k + 2) * w_time * (n_x + n_y - 2) / 2 + w_time, "far", 0, k))
    for _, kind, t, k in sorted(events):
        if kind == "a":
            pl.when(inner)(functools.partial(pass_acts, t, k))
        elif kind == "near":
            first_weights(k)
        else:
            far_weights(k)
    for k in range(n_w):
        for source in [pair] + [row_of(dy, dx, True) for dy, dx in peers_x + peers_y + diagonal]:
            wait_weight(source, k)

    def product(source, rows):
        at = lax.rem(source - c + n_col, n_col)
        return jnp.dot(acts[source, rows, :], weights[at], preferred_element_type=jnp.float32)

    own_a.wait()
    own_w.wait()
    every = pl.ds(0, tokens)
    total[...] = product(c, every)

    @pl.loop(0, last - 1)
    def _(t):
        source = source_at(t)

        @pl.when(jnp.logical_not(inner))
        def _():
            for k in range(n_a):
                act_copy(source, 0, k).wait_recv()

        total[...] += product(source, every)

    final = source_at(last - 1)

    @pl.loop(0, n_a)
    def _(k):
        rows = pl.ds(pl.multiple_of(k * row_a, row_a), row_a)

        @pl.when(jnp.logical_not(inner))
        def _():
            act_copy(final, 0, k).wait_recv()

        pre = total[rows, :] + product(final, rows)
        out[rows, :] = (pre / (1.0 + jnp.exp(-pre))).astype(out.dtype)

    for k in range(n_a):
        own_acts(k, lambda copy: copy.wait_send())

    @pl.when(inner)
    def _():
        @pl.loop(0, last)
        def _(t):
            source = source_at(t)
            for k in range(n_a):
                @pl.when(source < c)
                def _():
                    act_copy(source, 1, k).wait_send()

                @pl.when(source > c)
                def _():
                    act_copy(source, 0, k).wait_send()

    for k in range(n_w):
        for slot, to in enumerate(row_peers):
            weight_copy(r, to, slot, k, True).wait_send()
        relays(k, lambda copy: copy.wait_send())
        for n, source in enumerate(near + far):
            weight_copy(source, pair, base_share + n, k).wait_send()


def body(n_row, n_col, act_tiles, up_tiles):
    tokens, width = act_tiles.shape
    depth, hidden = up_tiles.shape
    chips = n_row // 2
    n_x = max(n for n in range(1, chips + 1) if chips % n == 0 and n * n <= chips)
    n_y = chips // n_x
    n_a, n_w = pieces_of(tokens, 4, 16), pieces_of(depth, 2, 16)
    sends = (n_x - 1) + (n_y - 1) + 1 + (n_x - 1) * (n_y - 1) + chips - 1
    return pl.pallas_call(
        functools.partial(kernel, (n_y, n_x, n_col), (n_a, n_w)),
        out_shape=pltpu.VMEM((tokens, hidden), jnp.bfloat16),
        in_specs=[pl.BlockSpec(memory_space=pltpu.HBM)] * 2,
        out_specs=pl.BlockSpec(memory_space=pltpu.VMEM),
        scratch_shapes=[
            pltpu.VMEM((n_col, tokens, width), jnp.bfloat16),
            pltpu.VMEM((n_row * depth // width, width, hidden), jnp.bfloat16),
            pltpu.VMEM((tokens, hidden), jnp.float32),
            pltpu.SemaphoreType.DMA((2, n_col, n_a)),
            pltpu.SemaphoreType.DMA((n_col, n_a)),
            pltpu.SemaphoreType.DMA((sends, n_w)),
            pltpu.SemaphoreType.DMA((n_row, n_w)),
            pltpu.SemaphoreType.DMA((2,)),
        ],
        compiler_params=pltpu.CompilerParams(collective_id=0, has_side_effects=True, vmem_limit_bytes=60000000),
        cost_estimate=pl.CostEstimate(
            flops=2 * tokens * width * n_col * hidden,
            bytes_accessed=2 * (act_tiles.size + up_tiles.size + tokens * hidden),
            transcendentals=tokens * hidden,
        ),
        name="gather_up_silu",
    )(act_tiles, up_tiles)


def solution(mesh):
    return jax.shard_map(
        functools.partial(body, mesh.shape["row"], mesh.shape["col"]),
        mesh=mesh,
        in_specs=(P("row", "col"), P("row", "col")),
        out_specs=P("row", "col"),
        check_vma=False,
    )
```

```python
import functools

import jax
import jax.numpy as jnp
from jax import lax
from jax.experimental import pallas as pl
from jax.experimental.pallas import tpu as pltpu
from jax.sharding import PartitionSpec as P

MESH = pl.DeviceIdType.MESH


def pieces_of(rows, wanted, multiple):
    return max(n for n in range(1, wanted + 1) if rows % (n * multiple) == 0)


def pieces_halved(rows, wanted, multiple):
    pieces = []
    while len(pieces) < wanted - 1 and rows % (2 * multiple) == 0:
        rows //= 2
        pieces.append(rows)
    return pieces + [rows]


def kernel(grid, counts, a_hbm, w_hbm, out, acts, weights, total, send_a, recv_a, send_w, recv_w, local_sem):
    n_y, n_x, n_col = grid
    n_a, n_w = counts
    n_row = 2 * n_y * n_x
    tokens, width = acts.shape[1:]
    depth = w_hbm.shape[0]
    per = width // depth
    row_w = depth // n_w
    starts_a = [sum(n_a[:k]) for k in range(len(n_a))]
    sizes_a, n_a = n_a, len(n_a)

    r, c = lax.axis_index("row"), lax.axis_index("col")
    core = lax.rem(r, 2)
    x = lax.rem(r // 2, n_x)
    y = r // (2 * n_x)
    last = n_col - 1

    def row_of(dy, dx, other_core=False):
        which = 1 - core if other_core else core
        return (lax.rem(y + dy, n_y) * n_x + lax.rem(x + dx, n_x)) * 2 + which

    pair = row_of(0, 0, True)
    peers_x = [(0, dx) for dx in range(1, n_x)]
    peers_y = [(dy, 0) for dy in range(1, n_y)]
    diagonal = [(dy, dx) for dy in range(1, n_y) for dx in range(1, n_x)]

    def weight_at(source, owner, k):
        rel = lax.rem(source - owner + n_row, n_row)
        return weights.at[rel // per, pl.ds(pl.multiple_of(lax.rem(rel, per) * depth + k * row_w, row_w), row_w)]

    def weight_copy(source, to, slot, k):
        return pltpu.make_async_remote_copy(
            src_ref=weight_at(source, r, k),
            dst_ref=weight_at(source, to, k),
            send_sem=send_w.at[slot, k],
            recv_sem=recv_w.at[source, k],
            device_id=(to, c),
            device_id_type=MESH,
        )

    def act_copy(source, side, k):
        return pltpu.make_async_remote_copy(
            src_ref=acts.at[source].at[pl.ds(starts_a[k], sizes_a[k])],
            dst_ref=acts.at[source, pl.ds(starts_a[k], sizes_a[k])],
            send_sem=send_a.at[side, source, k],
            recv_sem=recv_a.at[source, k],
            device_id=(r, c + 2 * side - 1),
            device_id_type=MESH,
        )

    own_a = pltpu.make_async_copy(a_hbm, acts.at[c], local_sem.at[0])
    own_w = pltpu.make_async_copy(w_hbm, weights.at[0, pl.ds(0, depth)], local_sem.at[1])
    own_a.start()
    own_w.start()

    barrier = pltpu.get_barrier_semaphore()
    row_peers = [row_of(*p) for p in peers_x + peers_y] + [pair]
    for to in row_peers:
        pl.semaphore_signal(barrier, inc=1, device_id=(to, c), device_id_type=MESH)

    @pl.when(c > 0)
    def _():
        pl.semaphore_signal(barrier, inc=1, device_id=(r, c - 1), device_id_type=MESH)

    @pl.when(c < last)
    def _():
        pl.semaphore_signal(barrier, inc=1, device_id=(r, c + 1), device_id_type=MESH)

    beside = jnp.where(c > 0, 1, 0) + jnp.where(c < last, 1, 0)
    pl.semaphore_wait(barrier, len(row_peers) + beside)

    def own_acts(k, act):
        @pl.when(c < last)
        def _():
            act(act_copy(c, 1, k))

        @pl.when(c > 0)
        def _():
            act(act_copy(c, 0, k))

    own_a.wait()
    for k in range(n_a):
        own_acts(k, lambda copy: copy.start())
    own_w.wait()
    for k in range(n_w):
        for slot, to in enumerate(row_peers):
            weight_copy(r, to, slot, k).start()

    near = [row_of(*p) for p in peers_x + peers_y]
    far = [row_of(*p) for p in diagonal]
    base_relay = len(row_peers)
    base_share = base_relay + len(diagonal)

    def relays(k, act):
        for n, (dy, dx) in enumerate(diagonal):
            @pl.when(core == 0)
            def _():
                act(weight_copy(row_of(dy, 0), row_of(0, dx), base_relay + n, k))

            @pl.when(core == 1)
            def _():
                act(weight_copy(row_of(0, dx), row_of(dy, 0), base_relay + n, k))

    def wait_weight(source, k):
        weight_copy(source, r, 0, k).wait_recv()

    def first_weights(k):
        for source in near:
            wait_weight(source, k)
        relays(k, lambda copy: copy.start())
        for n, source in enumerate(near):
            weight_copy(source, pair, base_share + n, k).start()

    def far_weights(k):
        for n, source in enumerate(far):
            wait_weight(source, k)
            weight_copy(source, pair, base_share + len(near) + n, k).start()

    short = jnp.minimum(c, last - c)
    toward = jnp.where(last - c >= c, 1, -1)

    def source_at(t):
        near_step = t // 2 + 1
        near_sign = toward * (1 - 2 * lax.rem(t, 2))
        return jnp.where(t < 2 * short, c + near_sign * near_step, c + toward * (t - short + 1))

    inner = jnp.logical_and(c > 0, c < last)

    def pass_acts(t, k):
        source = source_at(t)
        act_copy(source, 0, k).wait_recv()

        @pl.when(source < c)
        def _():
            act_copy(source, 1, k).start()

        @pl.when(source > c)
        def _():
            act_copy(source, 0, k).start()

    events = []
    a_time, w_time = tokens // n_a * width, row_w * weights.shape[2]
    for t in range(last):
        for k in range(n_a):
            events.append(((t // 2 * n_a + k + 1) * a_time, "a", t, k))
    for k in range(n_w):
        events.append(((k + 1) * w_time * (n_x + n_y - 2) / 2, "near", 0, k))
        events.append(((k + 2) * w_time * (n_x + n_y - 2) / 2 + w_time, "far", 0, k))
    for _, kind, t, k in sorted(events):
        if kind == "a":
            pl.when(inner)(functools.partial(pass_acts, t, k))
        elif kind == "near":
            first_weights(k)
        else:
            far_weights(k)
    for k in range(n_w):
        for source in [pair] + [row_of(dy, dx, True) for dy, dx in peers_x + peers_y + diagonal]:
            wait_weight(source, k)

    def product(source, rows):
        at = lax.rem(source - c + n_col, n_col)
        return jnp.dot(acts[source, rows, :], weights[at], preferred_element_type=jnp.float32)

    every = pl.ds(0, tokens)
    total[...] = product(c, every)

    @pl.loop(0, last - 1)
    def _(t):
        source = source_at(t)

        @pl.when(jnp.logical_not(inner))
        def _():
            for k in range(n_a):
                act_copy(source, 0, k).wait_recv()

        total[...] += product(source, every)

    final = source_at(last - 1)

    for k in range(n_a):
        rows = pl.ds(starts_a[k], sizes_a[k])

        pl.when(jnp.logical_not(inner))(act_copy(final, 0, k).wait_recv)

        pre = total[rows, :] + product(final, rows)
        out[rows, :] = (pre / (1.0 + jnp.exp(-pre))).astype(out.dtype)

    for k in range(n_a):
        own_acts(k, lambda copy: copy.wait_send())

    @pl.when(inner)
    def _():
        @pl.loop(0, last)
        def _(t):
            source = source_at(t)
            for k in range(n_a):
                @pl.when(source < c)
                def _():
                    act_copy(source, 1, k).wait_send()

                @pl.when(source > c)
                def _():
                    act_copy(source, 0, k).wait_send()

    for k in range(n_w):
        for slot, to in enumerate(row_peers):
            weight_copy(r, to, slot, k).wait_send()
        relays(k, lambda copy: copy.wait_send())
        for n, source in enumerate(near + far):
            weight_copy(source, pair, base_share + n, k).wait_send()


def body(n_row, n_col, act_tiles, up_tiles):
    tokens, width = act_tiles.shape
    depth, hidden = up_tiles.shape
    chips = n_row // 2
    n_x = max(n for n in range(1, chips + 1) if chips % n == 0 and n * n <= chips)
    n_y = chips // n_x
    cuts, n_w = pieces_halved(tokens, 3, 16), pieces_of(depth, 1, 16)
    n_a = len(cuts)
    sends = (n_x - 1) + (n_y - 1) + 1 + (n_x - 1) * (n_y - 1) + chips - 1
    return pl.pallas_call(
        functools.partial(kernel, (n_y, n_x, n_col), (cuts, n_w)),
        out_shape=pltpu.VMEM((tokens, hidden), jnp.bfloat16),
        in_specs=[pl.BlockSpec(memory_space=pltpu.HBM)] * 2,
        out_specs=pl.BlockSpec(memory_space=pltpu.VMEM),
        scratch_shapes=[
            pltpu.VMEM((n_col, tokens, width), jnp.bfloat16),
            pltpu.VMEM((n_row * depth // width, width, hidden), jnp.bfloat16),
            pltpu.VMEM((tokens, hidden), jnp.float32),
            pltpu.SemaphoreType.DMA((2, n_col, n_a)),
            pltpu.SemaphoreType.DMA((n_col, n_a)),
            pltpu.SemaphoreType.DMA((sends, n_w)),
            pltpu.SemaphoreType.DMA((n_row, n_w)),
            pltpu.SemaphoreType.DMA((2,)),
        ],
        compiler_params=pltpu.CompilerParams(collective_id=0, has_side_effects=True, vmem_limit_bytes=60000000),
        cost_estimate=pl.CostEstimate(
            flops=2 * tokens * width * n_col * hidden,
            bytes_accessed=2 * (act_tiles.size + up_tiles.size + tokens * hidden),
            transcendentals=tokens * hidden,
        ),
        name="gather_up_silu",
    )(act_tiles, up_tiles)


def solution(mesh):
    return jax.shard_map(
        functools.partial(body, mesh.shape["row"], mesh.shape["col"]),
        mesh=mesh,
        in_specs=(P("row", "col"), P("row", "col")),
        out_specs=P("row", "col"),
        check_vma=False,
    )
```

```python
import functools

import jax
import jax.numpy as jnp
from jax import lax
from jax.experimental import pallas as pl
from jax.experimental.pallas import tpu as pltpu
from jax.sharding import PartitionSpec as P

MESH = pl.DeviceIdType.MESH


def pieces_of(rows, wanted, multiple):
    return max(n for n in range(1, wanted + 1) if rows % (n * multiple) == 0)


def pieces_halved(rows, wanted, multiple):
    pieces = []
    while len(pieces) < wanted - 1 and rows % (2 * multiple) == 0:
        rows //= 2
        pieces.append(rows)
    return pieces + [rows]


def kernel(grid, counts, a_hbm, w_hbm, out, acts, weights, total, send_a, recv_a, send_w, recv_w, local_sem):
    n_y, n_x, n_col = grid
    n_a, n_w = counts
    n_row = 2 * n_y * n_x
    tokens, width = acts.shape[1:]
    depth = w_hbm.shape[0]
    per = width // depth
    row_w = depth // n_w
    starts_a = [sum(n_a[:k]) for k in range(len(n_a))]
    sizes_a, n_a = n_a, len(n_a)

    r, c = lax.axis_index("row"), lax.axis_index("col")
    core = lax.rem(r, 2)
    x = lax.rem(r // 2, n_x)
    y = r // (2 * n_x)
    last = n_col - 1

    def row_of(dy, dx, other_core=False):
        which = 1 - core if other_core else core
        return (lax.rem(y + dy, n_y) * n_x + lax.rem(x + dx, n_x)) * 2 + which

    pair = row_of(0, 0, True)
    peers_x = [(0, dx) for dx in range(1, n_x)]
    peers_y = [(dy, 0) for dy in range(1, n_y)]
    diagonal = [(dy, dx) for dy in range(1, n_y) for dx in range(1, n_x)]

    def weight_at(source, owner, k):
        rel = lax.rem(source - owner + n_row, n_row)
        return weights.at[rel // per, pl.ds(pl.multiple_of(lax.rem(rel, per) * depth + k * row_w, row_w), row_w)]

    def weight_copy(source, to, slot, k):
        return pltpu.make_async_remote_copy(
            src_ref=weight_at(source, r, k),
            dst_ref=weight_at(source, to, k),
            send_sem=send_w.at[slot, k],
            recv_sem=recv_w.at[source, k],
            device_id=(to, c),
            device_id_type=MESH,
        )

    def act_copy(source, side, k):
        return pltpu.make_async_remote_copy(
            src_ref=acts.at[source].at[pl.ds(starts_a[k], sizes_a[k])],
            dst_ref=acts.at[source, pl.ds(starts_a[k], sizes_a[k])],
            send_sem=send_a.at[side, source, k],
            recv_sem=recv_a.at[source, k],
            device_id=(r, c + 2 * side - 1),
            device_id_type=MESH,
        )

    own_a = pltpu.make_async_copy(a_hbm, acts.at[c], local_sem.at[0])
    own_w = pltpu.make_async_copy(w_hbm, weights.at[0, pl.ds(0, depth)], local_sem.at[1])
    own_a.start()
    own_w.start()

    barrier = pltpu.get_barrier_semaphore()
    row_peers = [row_of(*p) for p in peers_x + peers_y] + [pair]
    @pl.when(c > 0)
    def _():
        pl.semaphore_signal(barrier, inc=1, device_id=(r, c - 1), device_id_type=MESH)

    @pl.when(c < last)
    def _():
        pl.semaphore_signal(barrier, inc=1, device_id=(r, c + 1), device_id_type=MESH)

    for to in row_peers:
        pl.semaphore_signal(barrier, inc=1, device_id=(to, c), device_id_type=MESH)

    beside = jnp.where(c > 0, 1, 0) + jnp.where(c < last, 1, 0)
    pl.semaphore_wait(barrier, len(row_peers) + beside)

    def own_acts(k, act):
        @pl.when(c < last)
        def _():
            act(act_copy(c, 1, k))

        @pl.when(c > 0)
        def _():
            act(act_copy(c, 0, k))

    own_a.wait()
    for k in range(n_a):
        own_acts(k, lambda copy: copy.start())
    own_w.wait()
    for k in range(n_w):
        for slot, to in enumerate(row_peers):
            weight_copy(r, to, slot, k).start()

    near = [row_of(*p) for p in peers_x + peers_y]
    far = [row_of(*p) for p in diagonal]
    base_relay = len(row_peers)
    base_share = base_relay + len(diagonal)

    def relays(k, act):
        for n, (dy, dx) in enumerate(diagonal):
            @pl.when(core == 0)
            def _():
                act(weight_copy(row_of(dy, 0), row_of(0, dx), base_relay + n, k))

            @pl.when(core == 1)
            def _():
                act(weight_copy(row_of(0, dx), row_of(dy, 0), base_relay + n, k))

    def wait_weight(source, k):
        weight_copy(source, r, 0, k).wait_recv()

    def first_weights(k):
        for source in near:
            wait_weight(source, k)
        relays(k, lambda copy: copy.start())
        for n, source in enumerate(near):
            weight_copy(source, pair, base_share + n, k).start()

    def far_weights(k):
        for n, source in enumerate(far):
            wait_weight(source, k)
            weight_copy(source, pair, base_share + len(near) + n, k).start()

    short = jnp.minimum(c, last - c)
    toward = jnp.where(last - c >= c, 1, -1)

    def source_at(t):
        near_step = t // 2 + 1
        near_sign = toward * (1 - 2 * lax.rem(t, 2))
        return jnp.where(t < 2 * short, c + near_sign * near_step, c + toward * (t - short + 1))

    inner = jnp.logical_and(c > 0, c < last)

    def pass_acts(t, k):
        source = source_at(t)
        act_copy(source, 0, k).wait_recv()

        @pl.when(source < c)
        def _():
            act_copy(source, 1, k).start()

        @pl.when(source > c)
        def _():
            act_copy(source, 0, k).start()

    events = []
    a_time, w_time = tokens // n_a * width, row_w * weights.shape[2]
    for t in range(last):
        for k in range(n_a):
            events.append(((t // 2 * n_a + k + 1) * a_time, "a", t, k))
    for k in range(n_w):
        events.append(((k + 1) * w_time * (n_x + n_y - 2) / 2, "near", 0, k))
        events.append(((k + 2) * w_time * (n_x + n_y - 2) / 2 + w_time, "far", 0, k))
    for _, kind, t, k in sorted(events):
        if kind == "a":
            pl.when(inner)(functools.partial(pass_acts, t, k))
        elif kind == "near":
            first_weights(k)
        else:
            far_weights(k)
    for k in range(n_w):
        for source in [pair] + [row_of(dy, dx, True) for dy, dx in peers_x + peers_y + diagonal]:
            wait_weight(source, k)

    def product(source, rows):
        at = lax.rem(source - c + n_col, n_col)
        return jnp.dot(acts[source, rows, :], weights[at], preferred_element_type=jnp.float32)

    every = pl.ds(0, tokens)
    total[...] = product(c, every)

    @pl.loop(0, last - 1)
    def _(t):
        source = source_at(t)

        @pl.when(jnp.logical_not(inner))
        def _():
            for k in range(n_a):
                act_copy(source, 0, k).wait_recv()

        total[...] += product(source, every)

    final = source_at(last - 1)

    for k in range(n_a):
        rows = pl.ds(starts_a[k], sizes_a[k])

        pl.when(jnp.logical_not(inner))(act_copy(final, 0, k).wait_recv)

        pre = total[rows, :] + product(final, rows)
        out[rows, :] = (pre / (1.0 + jnp.exp(-pre))).astype(out.dtype)

    for k in range(n_a):
        own_acts(k, lambda copy: copy.wait_send())

    @pl.when(inner)
    def _():
        @pl.loop(0, last)
        def _(t):
            source = source_at(t)
            for k in range(n_a):
                @pl.when(source < c)
                def _():
                    act_copy(source, 1, k).wait_send()

                @pl.when(source > c)
                def _():
                    act_copy(source, 0, k).wait_send()

    for k in range(n_w):
        for slot, to in enumerate(row_peers):
            weight_copy(r, to, slot, k).wait_send()
        relays(k, lambda copy: copy.wait_send())
        for n, source in enumerate(near + far):
            weight_copy(source, pair, base_share + n, k).wait_send()


def body(n_row, n_col, act_tiles, up_tiles):
    tokens, width = act_tiles.shape
    depth, hidden = up_tiles.shape
    chips = n_row // 2
    n_x = max(n for n in range(1, chips + 1) if chips % n == 0 and n * n <= chips)
    n_y = chips // n_x
    cuts, n_w = pieces_halved(tokens, 3, 16), pieces_of(depth, 1, 16)
    n_a = len(cuts)
    sends = (n_x - 1) + (n_y - 1) + 1 + (n_x - 1) * (n_y - 1) + chips - 1
    return pl.pallas_call(
        functools.partial(kernel, (n_y, n_x, n_col), (cuts, n_w)),
        out_shape=pltpu.VMEM((tokens, hidden), jnp.bfloat16),
        in_specs=[pl.BlockSpec(memory_space=pltpu.HBM)] * 2,
        out_specs=pl.BlockSpec(memory_space=pltpu.VMEM),
        scratch_shapes=[
            pltpu.VMEM((n_col, tokens, width), jnp.bfloat16),
            pltpu.VMEM((n_row * depth // width, width, hidden), jnp.bfloat16),
            pltpu.VMEM((tokens, hidden), jnp.float32),
            pltpu.SemaphoreType.DMA((2, n_col, n_a)),
            pltpu.SemaphoreType.DMA((n_col, n_a)),
            pltpu.SemaphoreType.DMA((sends, n_w)),
            pltpu.SemaphoreType.DMA((n_row, n_w)),
            pltpu.SemaphoreType.DMA((2,)),
        ],
        compiler_params=pltpu.CompilerParams(collective_id=0, has_side_effects=True, vmem_limit_bytes=60000000),
        cost_estimate=pl.CostEstimate(
            flops=2 * tokens * width * n_col * hidden,
            bytes_accessed=2 * (act_tiles.size + up_tiles.size + tokens * hidden),
            transcendentals=tokens * hidden,
        ),
        name="gather_up_silu",
    )(act_tiles, up_tiles)


def solution(mesh):
    return jax.shard_map(
        functools.partial(body, mesh.shape["row"], mesh.shape["col"]),
        mesh=mesh,
        in_specs=(P("row", "col"), P("row", "col")),
        out_specs=P("row", "col"),
        check_vma=False,
    )
```
